768 devices in a mesh: seq: 12 (over x, z_lo), segment: 64 (over y, z_hi, core).
Axes of the slice: x: 4, y: 8, z: 12 (z_hi: 4, z_lo: 3; z = z_hi * 3 + z_lo), core: 2. Of those that a mesh axis runs over, the one named last changes fastest.
Arguments:
- stream: bfloat16 [1536, 32768], P('seq', 'segment'), may hold values from -6 to 6
- w_query: bfloat16 [4096, 16384], P(None, 'segment'), may hold values from -0.09375 to 0.09375
- w_out: bfloat16 [16384, 4096], P('segment'), may hold values from -0.125 to 0.125
- neighbour_kv: bfloat16 [2, 2, 6144, 16384], P(None, None, 'seq', 'segment'), may hold values from -6 to 6
Outputs:
- first: bfloat16 [1536, 32768], P('seq', 'segment')
- second: bfloat16 [1536, 32768], P('seq', 'segment')
The draws below stay inside these ranges and needn't reach their ends.
All inputs are finite; a program needn't handle non-finite values.
Results may differ from the reference program's by a relative error of at most 0.0075.
Values may be sent and summed in bfloat16 or wider, within the bound.
No kernel may reach another device: no remote copies, remote signals or barrier semaphores. Data moves between devices by JAX's collectives and lax.ppermute only.
A program may use at most 32 MiB of HBM per device.

```python
import jax
import jax.numpy as jnp
from jax import lax

D = 4096
HD = 128
HEADS = 16
SECT = 8
CH = 64
NEIGH = 2
NBL = 128
TICKS = 2
HG = 8
TOKENS = 1536
NBTOK = 6144


def steps_of(key, shape, cuts, low, largest):
    level = 1.0
    for position, parts in cuts:
        draws = jax.random.uniform(jax.random.fold_in(jax.random.fold_in(key, 6), position), (parts,), jnp.float32, low / len(cuts), largest / len(cuts))
        level = level * jnp.repeat(jnp.exp(draws), shape[position] // parts).reshape((-1,) + (1,) * (len(shape) - 1 - position))
    return level


def noise(stream_key, shape, width, bound, split=(), dtype=jnp.bfloat16):
    factor_of = steps_of(stream_key, shape, split, -0.22, 0.18) if split else 1.0
    values = jax.random.normal(stream_key, shape, jnp.float32) * width * factor_of
    return jnp.minimum(jnp.maximum(values, -bound), bound).astype(dtype)


def setup_inputs(seed: int = 0) -> dict:
    arg_keys = jax.random.split(jax.random.key(seed), 5)
    stream = noise(arg_keys[0], (TOKENS, SECT * D), 1.0, 6.0, ((0, 12), (1, 64)))
    w_query = noise(arg_keys[1], (D, SECT * HEADS * HD), D ** -0.5, 0.09375, ((1, 64),))
    w_out = noise(arg_keys[2], (SECT * HEADS * HD, D), (HEADS * HD) ** -0.5, 0.125, ((0, 64),))
    neighbour_kv = noise(arg_keys[3], (TICKS, 2, NBTOK, SECT * HEADS * HD), 1.0, 6.0, ((2, 12), (3, 64)))
    return dict(stream=stream, w_query=w_query, w_out=w_out, neighbour_kv=neighbour_kv)


EPS = 1e-05

def cross_layer(rows_in, keys_values, weight_query, weight_out):
    wide = rows_in.astype(jnp.float32)
    normed = (wide * lax.rsqrt(lax.optimization_barrier(jnp.mean(wide * wide, axis=-1, keepdims=True)) + EPS)).astype(jnp.bfloat16)
    queries = jnp.dot(normed, weight_query, preferred_element_type=jnp.float32).astype(jnp.bfloat16)
    tokens = queries.shape[0]
    spans = tokens // CH
    head_cols = HEADS * HD
    padded = jnp.concatenate([jnp.zeros((1, head_cols), jnp.bfloat16), queries, jnp.zeros((CH - 1, head_cols), jnp.bfloat16)], axis=0)
    grouped = padded.reshape(spans + 1, CH, HEADS, HD)[1:]
    keys = keys_values[0].reshape(spans, NEIGH * NBL, HEADS, HD)
    values = keys_values[1].reshape(spans, NEIGH * NBL, HEADS, HD)
    scores = jnp.einsum('gchd,gkhd->ghck', grouped.astype(jnp.float32), keys.astype(jnp.float32)) * HD ** (-0.5)
    exponent = jnp.exp(scores)
    weights = (exponent / lax.optimization_barrier(jnp.sum(exponent, axis=-1, keepdims=True))).astype(jnp.bfloat16)
    attended = jnp.einsum('ghck,gkhd->gchd', weights.astype(jnp.float32), values.astype(jnp.float32)).astype(jnp.bfloat16)
    attended = jnp.concatenate([jnp.zeros((1, CH, HEADS, HD), jnp.bfloat16), attended], axis=0)
    attended = attended.reshape(-1, head_cols)[1:1 + tokens]
    group_cols = head_cols // HG
    total = wide
    for group_no in range(HG):
        term = jnp.dot(attended[:, group_no * group_cols:(group_no + 1) * group_cols], weight_out[group_no * group_cols:(group_no + 1) * group_cols, :], preferred_element_type=jnp.float32).astype(jnp.bfloat16)
        term = lax.optimization_barrier(term)
        total = total + term.astype(jnp.float32)
    return total.astype(jnp.bfloat16)

def reference(stream, w_query, w_out, neighbour_kv):
    head_cols = HEADS * HD
    firsts = []
    for section in range(SECT):
        firsts.append(cross_layer(stream[:, section * D:(section + 1) * D], neighbour_kv[0][:, :, section * head_cols:(section + 1) * head_cols], w_query[:, section * head_cols:(section + 1) * head_cols], w_out[section * head_cols:(section + 1) * head_cols, :]))
    seconds = []
    for section in range(SECT):
        if section > 0:
            inputs = firsts[section - 1]
        else:
            inputs = jnp.zeros_like(firsts[0])
        seconds.append(cross_layer(inputs, neighbour_kv[1][:, :, section * head_cols:(section + 1) * head_cols], w_query[:, section * head_cols:(section + 1) * head_cols], w_out[section * head_cols:(section + 1) * head_cols, :]))
    return (jnp.concatenate(firsts, axis=1), jnp.concatenate(seconds, axis=1))
```

```python
import functools

import jax
import jax.numpy as jnp
from jax import lax
from jax.experimental import pallas as pl
from jax.experimental.pallas import tpu as pltpu
from jax.sharding import PartitionSpec as P

HD = 128
SECT = 8
CH = 64
SPAN = 256
EPS = 1e-05
CORES = 2


def z_route(size, per_section, step, sections_on=0, swap_core=False):
    route = []
    chips = per_section // CORES
    for source in range(size):
        section, group = divmod(source, per_section)
        chip, core = divmod(group, CORES)
        target_section = section + sections_on
        if target_section >= size // per_section:
            continue
        core = core ^ 1 if swap_core else core
        target = target_section * per_section + (chip + step) % chips * CORES + core
        route.append((source, target))
    return route


def along_z(block, step, sections_on=0, swap_core=False):
    size = lax.axis_size("segment")
    return lax.ppermute(block, "segment", z_route(size, size // SECT, step, sections_on, swap_core))


def along_seq(block, step):
    size = lax.axis_size("seq")
    return lax.ppermute(block, "seq", [(i, (i + step) % size) for i in range(size)])


def layer_kernel(chips, where_ref, x_refs, other_ref, wq_ref, kv_ref, wo_ref, mine_ref, send_ref):
    chip = where_ref[0]
    core = where_ref[1]
    masked = where_ref[2]
    rows = x_refs[0].shape[0]
    width = x_refs[0].shape[1]
    total = jnp.zeros((rows, 1), jnp.float32)
    queries = jnp.zeros((rows, wq_ref.shape[1]), jnp.float32)
    for k in range(chips):
        source = lax.rem(chip - k + chips, chips) * CORES
        for part, owner in ((x_refs[k][...], core), (other_ref[pl.ds(k * rows, rows), :], 1 - core)):
            wide = part.astype(jnp.float32)
            total += jnp.sum(wide * wide, axis=-1, keepdims=True)
            offset = pl.multiple_of((source + owner) * width, width)
            queries += jnp.dot(part, wq_ref[pl.ds(offset, width), :], preferred_element_type=jnp.float32)
    scale = lax.rsqrt(total / (2 * chips * width) + EPS)
    queries = (queries * scale).astype(jnp.bfloat16)
    heads = []
    for h in range(queries.shape[1] // HD):
        cols = slice(h * HD, (h + 1) * HD)
        scores = lax.dot_general(
            queries[:, cols], kv_ref[0, :, cols], (((1,), (1,)), ((), ())), preferred_element_type=jnp.float32
        ) * HD ** (-0.5)
        exponent = jnp.exp(scores)
        weights = (exponent / jnp.sum(exponent, axis=-1, keepdims=True)).astype(jnp.bfloat16)
        heads.append(jnp.dot(weights, kv_ref[1, :, cols], preferred_element_type=jnp.float32))
    attended = jnp.concatenate(heads, axis=1)
    row = lax.broadcasted_iota(jnp.int32, attended.shape, 0)
    attended = jnp.where((masked > 0) & (row < rows - 1), 0.0, attended).astype(jnp.bfloat16)
    for k in range(chips):
        target = lax.rem(chip + k, chips) * CORES
        for out_ref, owner in ((mine_ref, core), (send_ref, 1 - core)):
            offset = pl.multiple_of((target + owner) * width, width)
            out_ref[pl.ds(k * rows, rows), :] = jnp.dot(
                attended, wo_ref[:, pl.ds(offset, width)], preferred_element_type=jnp.float32
            ).astype(jnp.bfloat16)


def layer(where, blocks, other, w_query, kv, w_out):
    chips = len(blocks)
    rows, width = blocks[0].shape

    def body(where_ref, *refs):
        layer_kernel(chips, where_ref, refs[:chips], *refs[chips:])

    vmem = pl.BlockSpec(memory_space=pltpu.VMEM)
    shape = jax.ShapeDtypeStruct((chips * rows, width), jnp.bfloat16)
    return pl.pallas_call(
        body,
        in_specs=[pl.BlockSpec(memory_space=pltpu.SMEM)] + [vmem] * (chips + 4),
        out_specs=(vmem, vmem),
        out_shape=(shape, shape),
        cost_estimate=pl.CostEstimate(flops=300_000_000, bytes_accessed=10_000_000, transcendentals=40_000),
        name="layer",
    )(where, *blocks, other, w_query, kv, w_out)


def per_device(stream, w_query, w_out, neighbour_kv):
    per_section = lax.axis_size("segment") // SECT
    chips = per_section // CORES
    group = lax.axis_index("segment") % per_section
    seq = lax.axis_index("seq")
    last = (seq == lax.axis_size("seq") - 1).astype(jnp.int32)
    half = stream.shape[0] // 2
    top, low = stream[:half], stream[half:]
    row = lax.broadcasted_iota(jnp.int32, low.shape, 0)
    end = row == half - 1
    inputs = [jnp.where(end, top[half - 1 :], low)]
    inputs.append(jnp.where(end, low[half - 1 :], along_seq(top, -1)))
    outputs = [[], []]
    results = [None, None]
    for tick in range(2):
        for chunk in range(2):
            where = jnp.stack([group // CORES, group % CORES, last * chunk]).astype(jnp.int32)
            kv = neighbour_kv[tick, :, chunk * SPAN : (chunk + 1) * SPAN, :]
            if tick == 0:
                blocks = [inputs[chunk]] + [along_z(inputs[chunk], k) for k in range(1, chips)]
            else:
                blocks = [along_z(results[chunk], k, 1) for k in range(chips)]
            other = along_z(jnp.concatenate(blocks, axis=0), 0, 0, True)
            mine, send = layer(where, blocks, other, w_query, kv, w_out)
            received = along_z(send, 0, 0, True)
            total = mine.astype(jnp.float32) + received.astype(jnp.float32)
            sums = total.astype(jnp.bfloat16)
            rest = [along_z(sums[k * half : (k + 1) * half], k) for k in range(1, chips)]
            result = blocks[0].astype(jnp.float32) + total[:half]
            for part in rest:
                result = result + part.astype(jnp.float32)
            results[chunk] = result.astype(jnp.bfloat16)
        moved = along_seq(results[1], 1)
        outputs[tick] = jnp.concatenate(
            [jnp.where(end, results[0][half - 1 :], moved), jnp.where(end, results[1][half - 1 :], results[0])], axis=0
        )
    return tuple(outputs)


def solution(mesh):
    placed = (
        P("seq", "segment"),
        P(None, "segment"),
        P("segment", None),
        P(None, None, "seq", "segment"),
    )
    return jax.shard_map(
        per_device,
        mesh=mesh,
        in_specs=placed,
        out_specs=(P("seq", "segment"), P("seq", "segment")),
        check_vma=False,
    )
```

```python
import jax
import jax.numpy as jnp
from jax import lax
from jax.experimental import pallas as pl
from jax.experimental.pallas import tpu as pltpu
from jax.sharding import PartitionSpec as P

HD = 128
SECT = 8
SPAN = 256
EPS = 1e-05
CORES = 2


def chip_route(size, turn, step, sections_on):
    per_section = size // SECT
    chips = per_section // CORES
    route = []
    for source in range(size):
        section, group = divmod(source, per_section)
        chip, core = divmod(group, CORES)
        if section + sections_on >= SECT:
            continue
        ahead = step if core == 0 else -step
        target = (section + sections_on) * per_section + (chip + ahead) % chips * CORES + (core ^ turn)
        route.append((source, target))
    return route


def along_chips(block, step, sections_on=0):
    return lax.ppermute(block, "segment", chip_route(lax.axis_size("segment"), 0, step, sections_on))


def swap_cores(block):
    return lax.ppermute(block, "segment", chip_route(lax.axis_size("segment"), 1, 0, 0))


def edge_from_previous(block):
    spans, groups = lax.axis_size("seq"), lax.axis_size("segment")
    route = [
        (s * groups + g, (s + 1) * groups + g) for s in range(spans - 1) for g in range(groups) if g % CORES == 1
    ]
    return lax.ppermute(block, ("seq", "segment"), route)


def attend(queries, keys, values):
    scores = lax.dot_general(
        queries, keys, (((1,), (1,)), ((), ())), preferred_element_type=jnp.float32
    ) * HD ** (-0.5)
    exponent = jnp.exp(scores)
    weights = (exponent / jnp.sum(exponent, axis=-1, keepdims=True)).astype(jnp.bfloat16)
    return jnp.dot(weights, values, preferred_element_type=jnp.float32)


def layer_kernel(
    where_ref, own_ref, front_ref, back_ref, far_ref, wq0_ref, wq1_ref, main_ref, kv_ref, other_kv_ref, wo0_ref, wo1_ref,
    t_own_ref, t_front_ref, t_back_ref, t_far_ref,
):
    chip = where_ref[0]
    core = where_ref[1]
    chips = 4
    ahead = 1 - 2 * core
    rows, width = own_ref.shape
    total = jnp.zeros((rows, 1), jnp.float32)
    queries = [jnp.zeros((rows, wq0_ref.shape[1]), jnp.float32) for _ in range(CORES)]
    sources = (chip, chip - ahead, chip + ahead, chip + 2)
    for source, ref in zip(sources, (own_ref, front_ref, back_ref, far_ref)):
        part = ref[...]
        wide = part.astype(jnp.float32)
        total += jnp.sum(wide * wide, axis=-1, keepdims=True)
        offset = pl.multiple_of(lax.rem(source + chips, chips) * width, width)
        for i, wq_ref in enumerate((wq0_ref, wq1_ref)):
            queries[i] += jnp.dot(part, wq_ref[pl.ds(offset, width), :], preferred_element_type=jnp.float32)
    scale = lax.rsqrt(total / (chips * width) + EPS)
    last_row = lax.broadcasted_iota(jnp.int32, (16, HD), 0) == 15
    attended = []
    for i in range(CORES):
        q = (queries[i] * scale).astype(jnp.bfloat16)
        heads = []
        for h in range(q.shape[1] // HD):
            cols = slice(h * HD, (h + 1) * HD)
            main = attend(q[:, cols], main_ref[i, 0, :, cols], main_ref[i, 1, :, cols])
            if i == 0:
                keys, values = kv_ref[0, SPAN:, cols], kv_ref[1, SPAN:, cols]
            else:
                keys, values = other_kv_ref[0, :, cols], other_kv_ref[1, :, cols]
            end = attend(q[rows - 16 :, cols], keys, values)
            end = jnp.where(last_row & (core > 0), end, main[rows - 16 :])
            heads.append(jnp.concatenate([main[: rows - 16], end], axis=0))
        attended.append(jnp.concatenate(heads, axis=1).astype(jnp.bfloat16))
    targets = (chip + 2, chip - ahead, chip + ahead, chip)
    for target, ref in zip(targets, (t_far_ref, t_back_ref, t_front_ref, t_own_ref)):
        offset = pl.multiple_of(lax.rem(target + chips, chips) * width, width)
        term = jnp.dot(attended[0], wo0_ref[:, pl.ds(offset, width)], preferred_element_type=jnp.float32)
        term += jnp.dot(attended[1], wo1_ref[:, pl.ds(offset, width)], preferred_element_type=jnp.float32)
        ref[...] = term.astype(ref.dtype)


def layer(where, blocks, *operands):
    shape = blocks[0].shape
    vmem = pl.BlockSpec(memory_space=pltpu.VMEM)
    return pl.pallas_call(
        layer_kernel,
        in_specs=[pl.BlockSpec(memory_space=pltpu.SMEM)] + [vmem] * (len(blocks) + len(operands)),
        out_specs=(vmem,) * 4,
        out_shape=(jax.ShapeDtypeStruct(shape, jnp.float32),) + (jax.ShapeDtypeStruct(shape, jnp.bfloat16),) * 3,
        cost_estimate=pl.CostEstimate(flops=600_000_000, bytes_accessed=20_000_000, transcendentals=80_000),
        compiler_params=pltpu.CompilerParams(vmem_limit_bytes=24 << 20),
        name="layer",
    )(where, *blocks, *operands)


def per_device(stream, w_query, w_out, neighbour_kv):
    per_section = lax.axis_size("segment") // SECT
    group = lax.axis_index("segment") % per_section
    core = group % CORES
    first_core = core == 0
    where = jnp.stack([group // CORES, core]).astype(jnp.int32)
    half = stream.shape[0] // 2
    width = stream.shape[1]
    end = lax.broadcasted_iota(jnp.int32, (half, width), 0) == half - 1

    def trade_ends(top, low):
        return jnp.where(end, low[half - 1 :], top), jnp.where(end, top[half - 1 :], low)

    def by_core(here, there):
        return jnp.where(first_core, jnp.concatenate([here, there], axis=1), jnp.concatenate([there, here], axis=1))

    top, low = trade_ends(stream[:half], stream[half:])
    own = by_core(jnp.where(first_core, low, top), swap_cores(jnp.where(first_core, top, low)))

    near, far = neighbour_kv[:, :, :SPAN], neighbour_kv[:, :, SPAN:]
    other_kv = swap_cores(jnp.where(first_core, far, near))
    wq_other = swap_cores(w_query)
    wo_other = swap_cores(w_out)
    mains = []
    for tick in range(2):
        edge = edge_from_previous(jnp.stack([far[tick], other_kv[tick]]))
        mains.append(jnp.where(first_core, jnp.stack([near[tick], other_kv[tick]]), edge))

    outputs = []
    for tick in range(2):
        if tick == 0:
            front, back = along_chips(own, 1), along_chips(own, -1)
        else:
            front, back, own = along_chips(own, 1, 1), along_chips(own, -1, 1), along_chips(own, 0, 1)
        blocks = (own, front, back, along_chips(front, 1))
        t_own, t_front, t_back, t_far = layer(
            where, blocks, w_query, wq_other, mains[tick], neighbour_kv[tick], other_kv[tick], w_out, wo_other
        )
        passed = along_chips(t_far, 1)
        from_back = along_chips(t_back, -1)
        t_front = (t_front.astype(jnp.float32) + passed.astype(jnp.float32)).astype(jnp.bfloat16)
        from_front = along_chips(t_front, 1)
        result = own.astype(jnp.float32) + t_own + from_back.astype(jnp.float32) + from_front.astype(jnp.float32)
        own = result.astype(jnp.bfloat16)
        kept = jnp.where(first_core, own[:, :width], own[:, width:])
        moved = swap_cores(jnp.where(first_core, own[:, width:], own[:, :width]))
        out_top, out_low = trade_ends(jnp.where(first_core, moved, kept), jnp.where(first_core, kept, moved))
        outputs.append(jnp.concatenate([out_top, out_low], axis=0))
    return tuple(outputs)


def solution(mesh):
    placed = (
        P("seq", "segment"),
        P(None, "segment"),
        P("segment", None),
        P(None, None, "seq", "segment"),
    )
    return jax.shard_map(
        per_device,
        mesh=mesh,
        in_specs=placed,
        out_specs=(P("seq", "segment"), P("seq", "segment")),
        check_vma=False,
    )
```

```python
import functools

import jax
import jax.numpy as jnp
from jax import lax
from jax.experimental import pallas as pl
from jax.experimental.pallas import tpu as pltpu
from jax.sharding import PartitionSpec as P


HD = 128
SECT = 8
SPAN = 256
EPS = 1e-05
CORES = 2


def beside(chip, core):
    return chip ^ 1 if core == 0 else 3 - chip


def across(chip, core):
    return 3 - chip if core == 0 else chip ^ 1


def beside_of_other(chip, core):
    return beside(chip, 1 - core)


def here(chip, core):
    return chip


def permuted(block, place, sections_on=0, turn=0):
    size = lax.axis_size("segment")
    per_section = size // SECT
    assert per_section == 4 * CORES
    route = []
    for source in range(size - sections_on * per_section):
        section, group = divmod(source, per_section)
        chip, core = divmod(group, CORES)
        route.append((source, (section + sections_on) * per_section + place(chip, core) * CORES + (core ^ turn)))
    return lax.ppermute(block, "segment", route)


def swap_cores(block):
    return permuted(block, here, turn=1)


def from_previous(block):
    size = lax.axis_size("seq")
    return lax.ppermute(block, "seq", [(i, i + 1) for i in range(size - 1)])


def attend(queries, keys, values):
    scores = lax.dot_general(
        queries, keys, (((1,), (1,)), ((), ())), preferred_element_type=jnp.float32
    ) * HD ** (-0.5)
    exponent = jnp.exp(scores)
    weights = (exponent / jnp.sum(exponent, axis=-1, keepdims=True)).astype(jnp.bfloat16)
    return jnp.dot(weights, values, preferred_element_type=jnp.float32)


def add_queries(ref, sources, wq_refs, queries, total):
    rows, width = ref.shape[0] // 2, ref.shape[1]
    for i, source in enumerate(sources):
        part = ref[i * rows : (i + 1) * rows, :]
        wide = part.astype(jnp.float32)
        total += jnp.sum(wide * wide, axis=-1, keepdims=True)
        offset = pl.multiple_of(source * width, width)
        queries = [
            q + jnp.dot(part, wq_ref[pl.ds(offset, width), :], preferred_element_type=jnp.float32)
            for q, wq_ref in zip(queries, wq_refs)
        ]
    return queries, total


def put_terms(attended, targets, wo_refs, out_ref):
    rows, width = out_ref.shape[0] // 2, out_ref.shape[1]
    for i, target in enumerate(targets):
        offset = pl.multiple_of(target * width, width)
        cols = wo_refs[0].shape[0]
        term = sum(
            jnp.dot(attended[:, n * cols : (n + 1) * cols], wo_ref[:, pl.ds(offset, width)], preferred_element_type=jnp.float32)
            for n, wo_ref in enumerate(wo_refs)
        )
        out_ref[i * rows : (i + 1) * rows, :] = term.astype(out_ref.dtype)


def front_kernel(where_ref, pair_ref, wq0_ref, wq1_ref, queries_ref, total_ref):
    rows, cols = queries_ref.shape[0], wq0_ref.shape[1]
    queries = [jnp.zeros((rows, cols), jnp.float32) for _ in range(CORES)]
    total = jnp.zeros((rows, 1), jnp.float32)
    queries, total = add_queries(pair_ref, (where_ref[0], where_ref[1]), (wq0_ref, wq1_ref), queries, total)
    for i in range(CORES):
        queries_ref[:, i * cols : (i + 1) * cols] = queries[i]
    total_ref[...] = jnp.broadcast_to(total, total_ref.shape)


def middle_kernel(
    tick, where_ref, distant_ref, queries_ref, total_ref, wq0_ref, wq1_ref, kv_ref, edge_ref, other_ref, wo0_ref, wo1_ref,
    attended_ref, terms_ref,
):
    core = where_ref[4]
    rows, cols = attended_ref.shape[0], wq0_ref.shape[1]
    queries = [queries_ref[:, i * cols : (i + 1) * cols] for i in range(CORES)]
    distant = (where_ref[2], where_ref[3])
    queries, total = add_queries(distant_ref, distant, (wq0_ref, wq1_ref), queries, total_ref[:, :1])
    scale = lax.rsqrt(total / wq0_ref.shape[0] + EPS)
    last_row = lax.broadcasted_iota(jnp.int32, (16, HD), 0) == 15
    for i in range(CORES):
        q = (queries[i] * scale).astype(jnp.bfloat16)
        for h in range(cols // HD):
            head = slice(h * HD, (h + 1) * HD)
            out = slice(i * cols + h * HD, i * cols + (h + 1) * HD)
            if i == 0:
                mains = [jnp.where(core == 0, kv_ref[tick, n, :SPAN, head], edge_ref[n, :, head]) for n in range(2)]
                ends = [kv_ref[tick, n, SPAN:, head] for n in range(2)]
            else:
                mains = [other_ref[0, n, :, head] for n in range(2)]
                ends = [other_ref[1, n, :, head] for n in range(2)]
            main = attend(q[:, head], *mains)
            end = attend(q[rows - 16 :, head], *ends)
            end = jnp.where(last_row & (core > 0), end, main[rows - 16 :])
            attended_ref[: rows - 16, out] = main[: rows - 16].astype(jnp.bfloat16)
            attended_ref[rows - 16 :, out] = end.astype(jnp.bfloat16)
    put_terms(attended_ref[...], distant, (wo0_ref, wo1_ref), terms_ref)


def back_kernel(where_ref, attended_ref, wo0_ref, wo1_ref, terms_ref):
    put_terms(attended_ref[...], (where_ref[0], where_ref[1]), (wo0_ref, wo1_ref), terms_ref)


def pair_kernel(where_ref, mine_ref, moved_ref, beside_mine_ref, beside_given_ref, pair_ref):
    rows, width = mine_ref.shape
    first_core = where_ref[4] == 0
    for i, (own_ref, other_ref) in enumerate(((mine_ref, moved_ref), (beside_mine_ref, beside_given_ref))):
        own, other = own_ref[...], other_ref[...]
        pair_ref[i * rows : (i + 1) * rows, :width] = jnp.where(first_core, own, other)
        pair_ref[i * rows : (i + 1) * rows, width:] = jnp.where(first_core, other, own)


def join_kernel(where_ref, ours_ref, theirs_ref, pair_ref):
    rows = pair_ref.shape[0] // 2
    for i in range(2):
        here_rows, other_rows = slice(i * rows, (i + 1) * rows), slice((1 - i) * rows, (2 - i) * rows)
        total = ours_ref[here_rows, :].astype(jnp.float32) + theirs_ref[other_rows, :].astype(jnp.float32)
        pair_ref[here_rows, :] = total.astype(pair_ref.dtype)


def call(kernel, shapes, flops, nbytes, *operands):
    vmem = pl.BlockSpec(memory_space=pltpu.VMEM)
    return pl.pallas_call(
        kernel,
        in_specs=[pl.BlockSpec(memory_space=pltpu.SMEM)] + [vmem] * (len(operands) - 1),
        out_specs=(vmem,) * len(shapes),
        out_shape=tuple(jax.ShapeDtypeStruct(*shape) for shape in shapes),
        cost_estimate=pl.CostEstimate(flops=flops, bytes_accessed=nbytes, transcendentals=0),
        compiler_params=pltpu.CompilerParams(vmem_limit_bytes=12 << 20),
    )(*operands)


def per_device(stream, w_query, w_out, neighbour_kv):
    per_section = lax.axis_size("segment") // SECT
    group = lax.axis_index("segment") % per_section
    chip, core = group // CORES, group % CORES
    first_core = core == 0
    near = jnp.where(first_core, chip ^ 1, 3 - chip)
    far = jnp.where(first_core, 3 - chip, chip ^ 1)
    where = jnp.stack([chip, near, far, chip ^ 2, core]).astype(jnp.int32)
    half, width = stream.shape[0] // 2, stream.shape[1]
    end = lax.broadcasted_iota(jnp.int32, (half, width), 0) == half - 1
    low_first = first_core != end

    def features(block, wanted):
        return jnp.where(wanted, block[:, :width], block[:, width:])

    def arranged(own, other):
        return jnp.concatenate([jnp.where(low_first, other, own), jnp.where(low_first, own, other)], axis=0)

    top, low = stream[:half], stream[half:]
    mine = jnp.where(low_first, low, top)
    given = jnp.where(low_first, top, low)
    beside_mine = permuted(mine, beside)
    beside_given = permuted(given, beside_of_other, turn=1)
    moved = swap_cores(given)
    block = (2 * half, 2 * width)
    (pair,) = call(
        pair_kernel, ((block, jnp.bfloat16),), 0, 500_000, where, mine, moved, beside_mine, beside_given
    )

    edges = [from_previous(neighbour_kv[0, :, SPAN:])]
    later_kv, _ = lax.optimization_barrier((neighbour_kv, pair))
    near_kv, far_kv = later_kv[:, :, :SPAN], later_kv[:, :, SPAN:]
    edges.append(from_previous(far_kv[1]))
    wq_other = swap_cores(w_query)
    wo_other = swap_cores(w_out)

    for tick in range(2):
        distant = permuted(pair, across)
        given = jnp.where(first_core, jnp.stack([edges[tick], far_kv[tick]]), jnp.stack([near_kv[tick]] * 2))
        other_kv = swap_cores(given)
        wide = (half, 2 * wq_other.shape[1])
        queries, total = call(
            front_kernel, ((wide, jnp.float32), ((half, HD), jnp.float32)), 140_000_000, 3_000_000, where, pair, w_query, wq_other
        )
        attended, terms = call(
            functools.partial(middle_kernel, tick), ((wide, jnp.bfloat16), (block, jnp.bfloat16)), 350_000_000, 10_000_000,
            where, distant, queries, total, w_query, wq_other, neighbour_kv, edges[tick], other_kv, w_out, wo_other,
        )
        summed = permuted(terms, across)
        (terms,) = call(back_kernel, ((block, jnp.float32),), 140_000_000, 3_000_000, where, attended, w_out, wo_other)
        base = jnp.concatenate([pair[:half], jnp.zeros_like(pair[half:])], axis=0)
        part = (terms + summed.astype(jnp.float32) + base.astype(jnp.float32)).astype(jnp.bfloat16)
        own, theirs = part[:half], part[half:]
        if tick == 0:
            ours = permuted(part, beside, 1)
            pair = permuted(part, here, 1)
            (pair,) = call(join_kernel, ((block, jnp.bfloat16),), 0, 800_000, where, pair, ours)
            from_near = permuted(theirs, beside)
            own = (own.astype(jnp.float32) + from_near.astype(jnp.float32)).astype(jnp.bfloat16)
            other = swap_cores(features(own, core == 1))
            first = arranged(features(own, first_core), other)
        else:
            from_near = permuted(features(theirs, first_core), beside)
            other_near = permuted(features(theirs, core == 1), beside, turn=1)
            other = swap_cores(features(own, core == 1))
            own = features(own, first_core).astype(jnp.float32) + from_near.astype(jnp.float32)
            other = other.astype(jnp.float32) + other_near.astype(jnp.float32)
            second = arranged(own.astype(jnp.bfloat16), other.astype(jnp.bfloat16))
    return first, second


def solution(mesh):
    placed = (
        P("seq", "segment"),
        P(None, "segment"),
        P("segment", None),
        P(None, None, "seq", "segment"),
    )
    return jax.shard_map(
        per_device,
        mesh=mesh,
        in_specs=placed,
        out_specs=(P("seq", "segment"), P("seq", "segment")),
        check_vma=False,
    )
```

```python
import functools

import jax
import jax.numpy as jnp
from jax import lax
from jax.experimental import pallas as pl
from jax.experimental.pallas import tpu as pltpu
from jax.sharding import PartitionSpec as P


HD = 128
SECT = 8
SPAN = 256
EPS = 1e-05
CORES = 2


def beside(chip, core):
    return chip ^ 1 if core == 0 else 3 - chip


def across(chip, core):
    return 3 - chip if core == 0 else chip ^ 1


def beside_of_other(chip, core):
    return beside(chip, 1 - core)


def here(chip, core):
    return chip


def permuted(block, place, sections_on=0, turn=0):
    size = lax.axis_size("segment")
    per_section = size // SECT
    assert per_section == 4 * CORES
    route = []
    for source in range(size - sections_on * per_section):
        section, group = divmod(source, per_section)
        chip, core = divmod(group, CORES)
        route.append((source, (section + sections_on) * per_section + place(chip, core) * CORES + (core ^ turn)))
    return lax.ppermute(block, "segment", route)


def swap_cores(block):
    return permuted(block, here, turn=1)


def from_previous(block):
    size = lax.axis_size("seq")
    return lax.ppermute(block, "seq", [(i, i + 1) for i in range(size - 1)])


def attend(queries, keys, values):
    scores = lax.dot_general(
        queries, keys, (((1,), (1,)), ((), ())), preferred_element_type=jnp.float32
    ) * HD ** (-0.5)
    exponent = jnp.exp(scores)
    weights = (exponent / jnp.sum(exponent, axis=-1, keepdims=True)).astype(jnp.bfloat16)
    return jnp.dot(weights, values, preferred_element_type=jnp.float32)


def add_queries(ref, blocks, queries, total):
    rows = ref.shape[0] // 2
    for i, weights in enumerate(blocks):
        part = ref[i * rows : (i + 1) * rows, :]
        wide = part.astype(jnp.float32)
        total += jnp.sum(wide * wide, axis=-1, keepdims=True)
        queries = [q + jnp.dot(part, w(), preferred_element_type=jnp.float32) for q, w in zip(queries, weights)]
    return queries, total


def rows_of(ref, source, width):
    return lambda: ref[pl.ds(pl.multiple_of(source * width, width), width), :]


def put_terms(attended, targets, wo_refs, out_ref):
    rows, width = out_ref.shape[0] // 2, out_ref.shape[1]
    for i, target in enumerate(targets):
        offset = pl.multiple_of(target * width, width)
        cols = wo_refs[0].shape[0]
        term = sum(
            jnp.dot(attended[:, n * cols : (n + 1) * cols], wo_ref[:, pl.ds(offset, width)], preferred_element_type=jnp.float32)
            for n, wo_ref in enumerate(wo_refs)
        )
        out_ref[i * rows : (i + 1) * rows, :] = term.astype(out_ref.dtype)


def front_kernel(where_ref, pair_ref, wq0_ref, wq1_ref, queries_ref, total_ref):
    rows, cols = queries_ref.shape[0], wq0_ref.shape[1]
    width = pair_ref.shape[1]
    blocks = [[rows_of(wq_ref, where_ref[i], width) for wq_ref in (wq0_ref, wq1_ref)] for i in range(2)]
    queries = [jnp.zeros((rows, cols), jnp.float32) for _ in range(CORES)]
    total = jnp.zeros((rows, 1), jnp.float32)
    queries, total = add_queries(pair_ref, blocks, queries, total)
    for i in range(CORES):
        queries_ref[:, i * cols : (i + 1) * cols] = queries[i]
    total_ref[...] = jnp.broadcast_to(total, total_ref.shape)


def middle_kernel(
    tick, where_ref, distant_ref, queries_ref, total_ref, wq0_ref, wq1_ref, kv_ref, edge_ref, other_ref, wo0_ref, wo1_ref,
    attended_ref, terms_ref,
):
    core = where_ref[4]
    rows, cols = attended_ref.shape[0], wq0_ref.shape[1]
    queries = [queries_ref[:, i * cols : (i + 1) * cols] for i in range(CORES)]
    distant = (where_ref[2], where_ref[3])
    width = distant_ref.shape[1]
    blocks = [[rows_of(wq_ref, source, width) for wq_ref in (wq0_ref, wq1_ref)] for source in distant]
    queries, total = add_queries(distant_ref, blocks, queries, total_ref[:, :1])
    scale = lax.rsqrt(total / wq0_ref.shape[0] + EPS)
    last_row = lax.broadcasted_iota(jnp.int32, (16, HD), 0) == 15
    for i in range(CORES):
        q = (queries[i] * scale).astype(jnp.bfloat16)
        for h in range(cols // HD):
            head = slice(h * HD, (h + 1) * HD)
            out = slice(i * cols + h * HD, i * cols + (h + 1) * HD)
            if i == 0:
                mains = [jnp.where(core == 0, kv_ref[tick, n, :SPAN, head], edge_ref[n, :, head]) for n in range(2)]
                ends = [kv_ref[tick, n, SPAN:, head] for n in range(2)]
            else:
                mains = [other_ref[0, n, :, head] for n in range(2)]
                ends = [other_ref[1, n, :, head] for n in range(2)]
            main = attend(q[:, head], *mains)
            end = attend(q[rows - 16 :, head], *ends)
            end = jnp.where(last_row & (core > 0), end, main[rows - 16 :])
            attended_ref[: rows - 16, out] = main[: rows - 16].astype(jnp.bfloat16)
            attended_ref[rows - 16 :, out] = end.astype(jnp.bfloat16)
    put_terms(attended_ref[...], distant, (wo0_ref, wo1_ref), terms_ref)


def back_kernel(where_ref, attended_ref, wo0_ref, wo1_ref, terms_ref):
    put_terms(attended_ref[...], (where_ref[0], where_ref[1]), (wo0_ref, wo1_ref), terms_ref)


def pair_kernel(where_ref, mine_ref, moved_ref, beside_mine_ref, beside_given_ref, pair_ref):
    rows, width = mine_ref.shape
    first_core = where_ref[4] == 0
    for i, (own_ref, other_ref) in enumerate(((mine_ref, moved_ref), (beside_mine_ref, beside_given_ref))):
        own, other = own_ref[...], other_ref[...]
        pair_ref[i * rows : (i + 1) * rows, :width] = jnp.where(first_core, own, other)
        pair_ref[i * rows : (i + 1) * rows, width:] = jnp.where(first_core, other, own)


def join_kernel(where_ref, ours_ref, theirs_ref, pair_ref):
    rows = pair_ref.shape[0] // 2
    for i in range(2):
        here_rows, other_rows = slice(i * rows, (i + 1) * rows), slice((1 - i) * rows, (2 - i) * rows)
        total = ours_ref[here_rows, :].astype(jnp.float32) + theirs_ref[other_rows, :].astype(jnp.float32)
        pair_ref[here_rows, :] = total.astype(pair_ref.dtype)


def total_of(terms_ref, summed_ref, pair_ref, i):
    rows = terms_ref.shape[0] // 2
    rows = slice(i * rows, (i + 1) * rows)
    total = terms_ref[rows, :] + summed_ref[rows, :].astype(jnp.float32)
    return total + pair_ref[rows, :].astype(jnp.float32) if i == 0 else total


def first_sum_kernel(terms_ref, summed_ref, pair_ref, part_ref, theirs_ref):
    rows = theirs_ref.shape[0]
    part_ref[:rows, :] = total_of(terms_ref, summed_ref, pair_ref, 0).astype(part_ref.dtype)
    theirs = total_of(terms_ref, summed_ref, pair_ref, 1).astype(part_ref.dtype)
    part_ref[rows:, :] = theirs
    theirs_ref[...] = theirs


def last_sum_kernel(where_ref, terms_ref, summed_ref, pair_ref, kept_ref, given_ref, near_kept_ref, near_given_ref):
    width = kept_ref.shape[1]
    first_core = where_ref[4] == 0
    for i, (here_ref, there_ref) in enumerate(((kept_ref, given_ref), (near_kept_ref, near_given_ref))):
        total = total_of(terms_ref, summed_ref, pair_ref, i)
        left, right = total[:, :width], total[:, width:]
        here_ref[...] = jnp.where(first_core, left, right).astype(here_ref.dtype)
        there_ref[...] = jnp.where(first_core, right, left).astype(there_ref.dtype)


def call(kernel, shapes, flops, nbytes, *operands):
    vmem = pl.BlockSpec(memory_space=pltpu.VMEM)
    specs = [vmem] * len(operands)
    if operands[0].ndim == 1:
        specs[0] = pl.BlockSpec(memory_space=pltpu.SMEM)
    return pl.pallas_call(
        kernel,
        in_specs=specs,
        out_specs=(vmem,) * len(shapes),
        out_shape=tuple(jax.ShapeDtypeStruct(*shape) for shape in shapes),
        cost_estimate=pl.CostEstimate(flops=flops, bytes_accessed=nbytes, transcendentals=0),
        compiler_params=pltpu.CompilerParams(vmem_limit_bytes=12 << 20),
    )(*operands)


def per_device(stream, w_query, w_out, neighbour_kv):
    per_section = lax.axis_size("segment") // SECT
    group = lax.axis_index("segment") % per_section
    chip, core = group // CORES, group % CORES
    first_core = core == 0
    near = jnp.where(first_core, chip ^ 1, 3 - chip)
    far = jnp.where(first_core, 3 - chip, chip ^ 1)
    where = jnp.stack([chip, near, far, chip ^ 2, core]).astype(jnp.int32)
    half, width = stream.shape[0] // 2, stream.shape[1]
    end = lax.broadcasted_iota(jnp.int32, (half, width), 0) == half - 1
    low_first = first_core != end

    def features(block, wanted):
        return jnp.where(wanted, block[:, :width], block[:, width:])

    def arranged(own, other):
        return jnp.concatenate([jnp.where(low_first, other, own), jnp.where(low_first, own, other)], axis=0)

    top, low = stream[:half], stream[half:]
    mine = jnp.where(low_first, low, top)
    given = jnp.where(low_first, top, low)
    beside_mine = permuted(mine, beside)
    beside_given = permuted(given, beside_of_other, turn=1)
    moved = swap_cores(given)
    block = (2 * half, 2 * width)
    (pair,) = call(
        pair_kernel, ((block, jnp.bfloat16),), 0, 500_000, where, mine, moved, beside_mine, beside_given
    )

    edges = [from_previous(neighbour_kv[0, :, SPAN:])]
    later_kv, _ = lax.optimization_barrier((neighbour_kv, pair))
    near_kv, far_kv = later_kv[:, :, :SPAN], later_kv[:, :, SPAN:]
    edges.append(from_previous(far_kv[1]))
    wq_other = swap_cores(w_query)
    wo_other = swap_cores(w_out)

    for tick in range(2):
        distant = permuted(pair, across)
        given = jnp.where(first_core, jnp.stack([edges[tick], far_kv[tick]]), jnp.stack([near_kv[tick]] * 2))
        other_kv = swap_cores(given)
        wide = (half, 2 * wq_other.shape[1])
        queries, total = call(
            front_kernel, ((wide, jnp.float32), ((half, HD), jnp.float32)), 140_000_000, 3_000_000,
            where, pair, w_query, wq_other,
        )
        attended, terms = call(
            functools.partial(middle_kernel, tick), ((wide, jnp.bfloat16), (block, jnp.bfloat16)), 350_000_000, 10_000_000,
            where, distant, queries, total, w_query, wq_other, neighbour_kv, edges[tick], other_kv, w_out, wo_other,
        )
        summed = permuted(terms, across)
        (terms,) = call(back_kernel, ((block, jnp.float32),), 140_000_000, 3_000_000, where, attended, w_out, wo_other)
        if tick == 0:
            part, theirs = call(
                first_sum_kernel, ((block, jnp.bfloat16), ((half, 2 * width), jnp.bfloat16)), 0, 1_200_000, terms, summed, pair
            )
            pair = permuted(part, here, 1)
            ours = permuted(part, beside, 1)
            (pair,) = call(join_kernel, ((block, jnp.bfloat16),), 0, 800_000, where, pair, ours)
            from_near = permuted(theirs, beside)
            own = (part[:half].astype(jnp.float32) + from_near.astype(jnp.float32)).astype(jnp.bfloat16)
            other = swap_cores(features(own, core == 1))
            first = arranged(features(own, first_core), other)
        else:
            quarter = (half, width)
            kept, given, near_kept, near_given = call(
                last_sum_kernel, ((quarter, jnp.float32),) + ((quarter, jnp.bfloat16),) * 3, 0, 1_200_000, where, terms, summed, pair
            )
            from_near = permuted(near_kept, beside)
            other_near = permuted(near_given, beside, turn=1)
            other = swap_cores(given)
            own = kept + from_near.astype(jnp.float32)
            other = other.astype(jnp.float32) + other_near.astype(jnp.float32)
            second = arranged(own.astype(jnp.bfloat16), other.astype(jnp.bfloat16))
    return first, second


def solution(mesh):
    placed = (
        P("seq", "segment"),
        P(None, "segment"),
        P("segment", None),
        P(None, None, "seq", "segment"),
    )
    return jax.shard_map(
        per_device,
        mesh=mesh,
        in_specs=placed,
        out_specs=(P("seq", "segment"), P("seq", "segment")),
        check_vma=False,
    )
```
